32 devices in a mesh: shard: 2 (over x), tensor: 4 (over y, core), section: 4 (over z).
Axes of the slice: x: 2, y: 2, z: 4, core: 2. Of those that a mesh axis runs over, the one named last changes fastest.
Arguments:
- grad_kv: bfloat16 [16, 1024, 2048], P(('shard', 'section'), None, 'tensor'), may hold values from -65000 to 65000
- grad_gate: bfloat16 [16, 512, 2048], P(('shard', 'section'), None, 'tensor'), may hold values from -65000 to 65000
- grad_laurel: bfloat16 [16, 128, 2048], P(('shard', 'section'), None, 'tensor'), may hold values from -65000 to 65000
- master_kv: float32 [1024, 2048], P(('shard', 'section'), 'tensor'), may hold values from -0.1 to 0.1
- master_gate: float32 [512, 2048], P(('shard', 'section'), 'tensor'), may hold values from -0.1 to 0.1
- master_laurel: float32 [128, 2048], P(('shard', 'section'), 'tensor'), may hold values from -0.1 to 0.1
- moment_kv: float32 [1024, 2048], P(('shard', 'section'), 'tensor'), may hold values from -0.1 to 0.1
- moment_gate: float32 [512, 2048], P(('shard', 'section'), 'tensor'), may hold values from -0.1 to 0.1
- moment_laurel: float32 [128, 2048], P(('shard', 'section'), 'tensor'), may hold values from -0.1 to 0.1
- second_kv: float32 [1024, 2048], P(('shard', 'section'), 'tensor'), may hold values from 0.01 to 1
- second_gate: float32 [512, 2048], P(('shard', 'section'), 'tensor'), may hold values from 0.01 to 1
- second_laurel: float32 [128, 2048], P(('shard', 'section'), 'tensor'), may hold values from 0.01 to 1
Outputs:
- new_master_kv: float32 [1024, 2048], P(('shard', 'section'), 'tensor')
- new_master_gate: float32 [512, 2048], P(('shard', 'section'), 'tensor')
- new_master_laurel: float32 [128, 2048], P(('shard', 'section'), 'tensor')
- new_moment_kv: float32 [1024, 2048], P(('shard', 'section'), 'tensor')
- new_moment_gate: float32 [512, 2048], P(('shard', 'section'), 'tensor')
- new_moment_laurel: float32 [128, 2048], P(('shard', 'section'), 'tensor')
- new_second_kv: float32 [1024, 2048], P(('shard', 'section'), 'tensor')
- new_second_gate: float32 [512, 2048], P(('shard', 'section'), 'tensor')
- new_second_laurel: float32 [128, 2048], P(('shard', 'section'), 'tensor')
- weights_kv: bfloat16 [1024, 2048], P(None, 'tensor')
- weights_gate: bfloat16 [512, 2048], P(None, 'tensor')
- weights_laurel: bfloat16 [128, 2048], P(None, 'tensor')
The draws below stay inside these ranges and needn't reach their ends.
All inputs are finite; a program needn't handle non-finite values.
Results may differ from the reference program's by a relative error of at most 0.015.
Values may be sent and summed in bfloat16 or wider, within the bound.
A program may use at most 64 MiB of HBM per device.

```python
import math
import jax
import jax.numpy as jnp
from jax import lax

D = 2048
KVW = 512
PLG = 256
RANK = 64
MB = 2
STEP = 10
REPL = 8


def gradient_draw(key, offset, row_count, plain_mix, target):
    key = jax.random.fold_in(key, offset)
    subkeys = jax.random.split(key, 6)
    copies = REPL * MB
    own_weight = plain_mix[0]
    shared_weight = plain_mix[1]
    own_part = jax.random.normal(subkeys[0], (copies, row_count, D), jnp.float32)
    shared_part = jax.random.normal(subkeys[5], (1, row_count, D), jnp.float32)
    sample = jnp.clip(own_weight * own_part + shared_weight * shared_part, -6.0, 6.0)
    spread = target / math.sqrt(own_weight * own_weight * copies + shared_weight * shared_weight * copies * copies)
    row_scale = jnp.exp(jax.random.uniform(subkeys[1], (row_count, 1), jnp.float32) * math.log(10.0))
    col_scale = jnp.exp(jax.random.uniform(subkeys[2], (1, D), jnp.float32) * math.log(10.0))
    row_rise = jnp.exp(jnp.arange(row_count, dtype=jnp.float32)[:, None] * (math.log(3.0) / row_count))
    col_rise = jnp.exp(jnp.arange(D, dtype=jnp.float32)[None, :] * (math.log(3.0) / D))
    owners = jax.random.permutation(subkeys[3], REPL)
    row_block = jnp.arange(row_count) // (row_count // REPL)
    replica = jnp.arange(copies) // MB
    boosted = 1.0 + 3.0 * (owners[replica][:, None] == row_block[None, :]).astype(jnp.float32)
    result = spread * sample * boosted[:, :, None] * row_scale * col_scale * row_rise * col_rise
    return result.astype(jnp.bfloat16)


def draw_grad_kv(key, part):
    return gradient_draw(key, 11, 2 * KVW, (1.0, 0.0), 1.0)


def draw_grad_gate(key, part):
    return gradient_draw(key, 23, 2 * PLG, (0.1, 1.0), 1.75)


def draw_grad_laurel(key, part):
    return gradient_draw(key, 37, 2 * RANK, (1.0, 0.25), 4.0)


def steps_of(key, dims, cuts, low, high):
    def one(dim, blocks):
        draws = jax.random.uniform(jax.random.fold_in(jax.random.fold_in(key, 6), dim), (blocks,), jnp.float32, low / len(cuts), high / len(cuts))
        return jnp.repeat(jnp.exp(draws), dims[dim] // blocks).reshape((-1,) + (1,) * (len(dims) - dim - 1))

    level = one(*cuts[0])
    for cut in cuts[1:]:
        level = level * one(*cut)
    return level


def setup_inputs(seed: int = 0) -> dict:
    key_of = jax.random.split(jax.random.key(seed), 13)
    return {
        "grad_kv": draw_grad_kv(jax.random.fold_in(key_of[12], 71), 0),
        "grad_gate": draw_grad_gate(jax.random.fold_in(key_of[12], 71), 0),
        "grad_laurel": draw_grad_laurel(jax.random.fold_in(key_of[12], 71), 0),
        "master_kv": jnp.clip(jax.random.uniform(key_of[3], (2 * KVW, D), jnp.float32, -0.1, 0.1) * steps_of(key_of[3], (2 * KVW, D), ((0, 8), (1, 4)), -0.4, 0.0), -0.1, 0.1),
        "master_gate": jnp.clip(jax.random.uniform(key_of[4], (2 * PLG, D), jnp.float32, -0.1, 0.1) * steps_of(key_of[4], (2 * PLG, D), ((0, 8), (1, 4)), -0.4, 0.0), -0.1, 0.1),
        "master_laurel": jnp.clip(jax.random.uniform(key_of[5], (2 * RANK, D), jnp.float32, -0.1, 0.1) * steps_of(key_of[5], (2 * RANK, D), ((0, 8), (1, 4)), -0.4, 0.0), -0.1, 0.1),
        "moment_kv": jnp.clip(jax.random.uniform(key_of[6], (2 * KVW, D), jnp.float32, -0.1, 0.1) * steps_of(key_of[6], (2 * KVW, D), ((0, 8), (1, 4)), -0.4, 0.0), -0.1, 0.1),
        "moment_gate": jnp.clip(jax.random.uniform(key_of[7], (2 * PLG, D), jnp.float32, -0.1, 0.1) * steps_of(key_of[7], (2 * PLG, D), ((0, 8), (1, 4)), -0.4, 0.0), -0.1, 0.1),
        "moment_laurel": jnp.clip(jax.random.uniform(key_of[8], (2 * RANK, D), jnp.float32, -0.1, 0.1) * steps_of(key_of[8], (2 * RANK, D), ((0, 8), (1, 4)), -0.4, 0.0), -0.1, 0.1),
        "second_kv": jnp.clip(jnp.exp(math.log(1.0) - 4.6051702 * jax.random.uniform(key_of[9], (2 * KVW, D), jnp.float32) ** steps_of(key_of[9], (2 * KVW, D), ((0, 8), (1, 4)), -0.2, 0.2)), 0.01, 1.0),
        "second_gate": jnp.clip(jnp.exp(math.log(1.0) - 4.6051702 * jax.random.uniform(key_of[10], (2 * PLG, D), jnp.float32) ** steps_of(key_of[10], (2 * PLG, D), ((0, 8), (1, 4)), -0.2, 0.2)), 0.01, 1.0),
        "second_laurel": jnp.clip(jnp.exp(math.log(1.0) - 4.6051702 * jax.random.uniform(key_of[11], (2 * RANK, D), jnp.float32) ** steps_of(key_of[11], (2 * RANK, D), ((0, 8), (1, 4)), -0.2, 0.2)), 0.01, 1.0),
    }


beta_one = 0.9
beta_two = 0.95
adam_eps = 1e-08
learn_rate = 0.05
weight_decay = 0.1
clip_rms = 0.5

def adamw_group(master, moment, second, summed, factor):
    clipped = factor * summed
    moment_new = beta_one * moment + (1.0 - beta_one) * clipped
    second_new = beta_two * second + (1.0 - beta_two) * clipped * clipped
    first_hat = moment_new / (1.0 - beta_one ** STEP)
    second_hat = second_new / (1.0 - beta_two ** STEP)
    master_new = master - learn_rate * (first_hat / (jnp.sqrt(second_hat) + adam_eps) + weight_decay * master)
    return (master_new, moment_new, second_new)

def reference(grad_kv, grad_gate, grad_laurel, master_kv, master_gate, master_laurel, moment_kv, moment_gate, moment_laurel, second_kv, second_gate, second_laurel):
    sums_all = [lax.optimization_barrier(jnp.sum(gradient, axis=0, dtype=jnp.float32)) for gradient in (grad_kv, grad_gate, grad_laurel)]
    squares = jnp.sum(sums_all[0] * sums_all[0]) + jnp.sum(sums_all[1] * sums_all[1]) + jnp.sum(sums_all[2] * sums_all[2])
    entries = sums_all[0].size + sums_all[1].size + sums_all[2].size
    ceiling = clip_rms * math.sqrt(entries)
    factor = ceiling / jnp.maximum(jnp.sqrt(squares), ceiling)
    kv_out = adamw_group(master_kv, moment_kv, second_kv, sums_all[0], factor)
    gate_out = adamw_group(master_gate, moment_gate, second_gate, sums_all[1], factor)
    laurel_out = adamw_group(master_laurel, moment_laurel, second_laurel, sums_all[2], factor)
    return (kv_out[0], gate_out[0], laurel_out[0], kv_out[1], gate_out[1], laurel_out[1], kv_out[2], gate_out[2], laurel_out[2], kv_out[0].astype(jnp.bfloat16), gate_out[0].astype(jnp.bfloat16), laurel_out[0].astype(jnp.bfloat16))
```

```python
import functools
import math

import jax
import jax.numpy as jnp
from jax import lax
from jax.experimental import pallas as pl
from jax.experimental.pallas import tpu as pltpu
from jax.sharding import PartitionSpec as P

STEP = 10

beta_one = 0.9
beta_two = 0.95
adam_eps = 1e-08
learn_rate = 0.05
weight_decay = 0.1
clip_rms = 0.5

WIRE = jnp.bfloat16
VMEM_LIMIT = 56 * 1024 * 1024
PIECE_ROWS = 32
DIRECT_DEVICES = 64
MESH = pl.DeviceIdType.MESH


def adamw_group(master, moment, second, summed, factor):
    clipped = factor * summed
    moment_new = beta_one * moment + (1.0 - beta_one) * clipped
    second_new = beta_two * second + (1.0 - beta_two) * clipped * clipped
    first_hat = moment_new / (1.0 - beta_one**STEP)
    second_hat = second_new / (1.0 - beta_two**STEP)
    master_new = master - learn_rate * (
        first_hat / (jnp.sqrt(second_hat) + adam_eps) + weight_decay * master
    )
    return (master_new, moment_new, second_new)


def cut(rows):
    starts = [sum(rows[:g]) for g in range(3)]
    if any(r % 16 for r in rows):
        parts = [(g, 0, rows[g]) for g in range(3)]
        return [(0, sum(rows), parts)], ()
    pieces = []
    for g in range(3):
        for first in range(0, rows[g], PIECE_ROWS):
            count = min(PIECE_ROWS, rows[g] - first)
            pieces.append((starts[g] + first, count, [(g, first, count)]))
    crossed = (len(pieces) - 2,) if len(pieces) > 4 else ()
    return pieces, crossed


def kernel(sizes, rows, batches, ceiling, *refs):
    shards, sections, tensors = sizes
    grads, states = refs[0:3], refs[3:12]
    new_states, weights = refs[12:21], refs[21]
    grad_buf, state_buf = refs[22:25], refs[25:34]
    (
        x_out, x_in, z_out, z_in, k_out, k_in, total,
        norm_out, norm_in, norm_mid, load_sem, state_sem,
        x_send, x_recv, z_send, z_recv, k_send, k_recv, norm_send, norm_recv,
        gx_send, gx_recv, gz_send, gz_recv,
    ) = refs[34:]
    s, t, z = lax.axis_index("shard"), lax.axis_index("tensor"), lax.axis_index("section")
    last = sections - 1
    pieces, crossed = cut(rows)
    plain = [c for c in range(len(pieces)) if c not in crossed]
    planes = range(shards)
    others = range(1, shards)

    def shard_at(j):
        return lax.rem(s + j, shards)

    def span(ref, c):
        return ref.at[pl.ds(pieces[c][0], pieces[c][1])]

    lo, hi = jnp.int32(0), jnp.int32(last)
    order = []
    for _ in range(sections):
        high = hi - z > z - lo
        order.append(jnp.where(high, hi, lo))
        lo, hi = jnp.where(high, lo, lo + 1), jnp.where(high, hi - 1, hi)

    loads = {}
    for j in list(others) + [0]:
        for k in range(sections):
            for g in range(3):
                copy = pltpu.make_async_copy(
                    grads[g].at[:, shard_at(j), order[k]], grad_buf[g].at[:, j, k], load_sem.at[j, k, g]
                )
                copy.start()
                loads[j, k, g] = copy

    barrier = pltpu.get_barrier_semaphore()
    everyone = [(a, c, b) for b in range(sections) for a in range(shards) for c in range(tensors)][1:]
    if shards * sections * tensors <= DIRECT_DEVICES:
        rounds = [everyone]
    else:
        rounds = [[e for e in everyone if e[1] == 0], [e for e in everyone if e[0] == 0 and e[2] == 0]]

    def device(a, c, b):
        return {
            "shard": shard_at(a), "tensor": lax.rem(t + c, tensors), "section": lax.rem(z + b, sections),
        }

    greeted = [e for r in rounds for e in r]
    for e in greeted:
        pl.semaphore_signal(barrier, inc=1, device_id=device(*e), device_id_type=MESH)

    state_loads = []
    for i in range(9):
        copy = pltpu.make_async_copy(states[i], state_buf[i], state_sem.at[i])
        copy.start()
        state_loads.append(copy)

    waited = set()

    def partial(j, k, c):
        out = []
        for g, first, count in pieces[c][2]:
            if (j, k, g) not in waited:
                loads[j, k, g].wait()
                waited.add((j, k, g))
            value = grad_buf[g][0, j, k, first : first + count].astype(jnp.float32)
            for m in range(1, batches):
                value = value + grad_buf[g][m, j, k, first : first + count].astype(jnp.float32)
            out.append(value)
        return out

    def parts(c):
        start = pieces[c][0]
        out = []
        for _, _, count in pieces[c][2]:
            out.append(slice(start, start + count))
            start += count
        return out

    def x_copy(j, k, c):
        return pltpu.make_async_remote_copy(
            src_ref=span(x_out.at[j - 1, k], c),
            dst_ref=span(x_in.at[j - 1, k], c),
            send_sem=x_send.at[j - 1, k, c],
            recv_sem=x_recv.at[j - 1, k, c],
            device_id={"shard": shard_at(j)},
            device_id_type=MESH,
        )

    greeting = True
    for k in range(sections):
        for j in others:
            for c in plain:
                for where, value in zip(parts(c), partial(j, k, c)):
                    x_out[j - 1, k, where] = value.astype(WIRE)
                if greeting:
                    pl.semaphore_wait(barrier, len(greeted))
                    greeting = False
                x_copy(j, k, c).start()

    @pl.when(z == 0)
    def _():
        z_in[0] = jnp.zeros(z_in.shape[1:], WIRE)

    @pl.when(z == last)
    def _():
        z_in[1] = jnp.zeros(z_in.shape[1:], WIRE)

    def z_wait(side, j, section, c):
        place = span(z_in.at[side, j, section], c)
        pltpu.make_async_remote_copy(
            src_ref=place,
            dst_ref=place,
            send_sem=z_send.at[0, 0, 0],
            recv_sem=z_recv.at[side, j, section, c],
            device_id={"section": z},
            device_id_type=MESH,
        ).wait_recv()

    def z_copy(j, k, c):
        up = (order[k] > z).astype(jnp.int32)
        side = 1 - up
        return pltpu.make_async_remote_copy(
            src_ref=span(z_out.at[j, k], c),
            dst_ref=span(z_in.at[side, j, order[k]], c),
            send_sem=z_send.at[j, k, c],
            recv_sem=z_recv.at[side, j, order[k], c],
            device_id={"section": z + 2 * up - 1},
            device_id_type=MESH,
        )

    def x_wait(k, c):
        for j in others:
            x_copy(j, k, c).wait_recv()

    inner = jnp.logical_and(z > 0, z < last)

    def z_step(k, c, among):
        for j in among:
            values = partial(j, k, c)
            if c in plain:
                x_wait(k, c)
                for i in others:
                    values = [v + x_in[i - 1, k, w].astype(jnp.float32) for v, w in zip(values, parts(c))]
            side = 1 - (order[k] > z).astype(jnp.int32)

            @pl.when(inner)
            def _():
                z_wait(side, j, order[k], c)

            for where, value in zip(parts(c), values):
                value = value + z_in[side, j, order[k], where].astype(jnp.float32)
                z_out[j, k, where] = value.astype(WIRE)
            z_copy(j, k, c).start()

    for k in range(last):
        for c in crossed:
            z_step(k, c, planes)
        for c in plain:
            z_step(k, c, [0])

    def arrived(j, c):
        values = partial(j, last, c)

        @pl.when(z > 0)
        def _():
            z_wait(0, j, z, c)

        @pl.when(z < last)
        def _():
            z_wait(1, j, z, c)

        return [
            v + z_in[0, j, z, w].astype(jnp.float32) + z_in[1, j, z, w].astype(jnp.float32)
            for v, w in zip(values, parts(c))
        ]

    def k_copy(j, c):
        return pltpu.make_async_remote_copy(
            src_ref=span(k_out.at[j - 1], c),
            dst_ref=span(k_in.at[j - 1], c),
            send_sem=k_send.at[j - 1, c],
            recv_sem=k_recv.at[j - 1, c],
            device_id={"shard": shard_at(j)},
            device_id_type=MESH,
        )

    for c in crossed:
        for j in others:
            for where, value in zip(parts(c), arrived(j, c)):
                k_out[j - 1, where] = value.astype(WIRE)
            k_copy(j, c).start()

    squares = jnp.zeros((1, total.shape[1]), jnp.float32)
    for c in plain:
        values = arrived(0, c)
        x_wait(last, c)
        for where, value in zip(parts(c), values):
            for j in others:
                value = value + x_in[j - 1, last, where].astype(jnp.float32)
            total[where] = value
            squares = squares + jnp.sum(value * value, axis=0, keepdims=True)
    for c in crossed:
        values = arrived(0, c)
        for j in others:
            k_copy(j, c).wait_recv()
        for where, value in zip(parts(c), values):
            for j in others:
                value = value + k_in[j - 1, where].astype(jnp.float32)
            total[where] = value
            squares = squares + jnp.sum(value * value, axis=0, keepdims=True)

    value = sum(squares[:, c : c + 128] for c in range(0, squares.shape[1], 128))
    slot = 0
    tail = []
    for r, group in enumerate(rounds):
        source = norm_out if r == 0 else norm_mid
        source[...] = value
        copies = []
        for e in group:
            copy = pltpu.make_async_remote_copy(
                src_ref=source,
                dst_ref=norm_in.at[slot],
                send_sem=norm_send.at[slot],
                recv_sem=norm_recv.at[slot],
                device_id=device(*e),
                device_id_type=MESH,
            )
            copy.start()
            copies.append((slot, copy))
            slot += 1
        if r == 0:
            for copy in state_loads:
                copy.wait()
            for k in range(sections):
                for j in others:
                    for c in plain:
                        x_copy(j, k, c).wait_send()
            for k in range(last):
                for c in crossed:
                    for j in planes:
                        z_copy(j, k, c).wait_send()
                for c in plain:
                    z_copy(0, k, c).wait_send()
            for c in crossed:
                for j in others:
                    k_copy(j, c).wait_send()
        for i, copy in copies:
            copy.wait_recv()
            value = value + norm_in[i]
        tail += [copy for _, copy in copies]
    norm = jnp.sqrt(jnp.sum(value, axis=1, keepdims=True))
    factor = ceiling / jnp.maximum(norm, ceiling)

    def gx_copy(j, plane, section, c):
        place = span(weights.at[plane, section], c)
        return pltpu.make_async_remote_copy(
            src_ref=place,
            dst_ref=place,
            send_sem=gx_send.at[j - 1, section, c],
            recv_sem=gx_recv.at[j - 1, section, c],
            device_id={"shard": shard_at(j)},
            device_id_type=MESH,
        )

    def gz_copy(side, j, section, c):
        place = span(weights.at[shard_at(j), section], c)
        return pltpu.make_async_remote_copy(
            src_ref=place,
            dst_ref=place,
            send_sem=gz_send.at[side, j, section, c],
            recv_sem=gz_recv.at[j, section, c],
            device_id={"section": z + 1 - 2 * side},
            device_id_type=MESH,
        )

    def spread(section, c):
        for j in others:
            gx_copy(j, s, section, c).start()

    def both(j, c, act):
        @pl.when(z < last)
        def _():
            act(gz_copy(0, j, z, c))

        @pl.when(z > 0)
        def _():
            act(gz_copy(1, j, z, c))

    def start(copy):
        copy.start()

    def finished(copy):
        copy.wait_send()

    def update(c):
        for (g, first, count), where in zip(pieces[c][2], parts(c)):
            rows_of = slice(first, first + count)
            new = adamw_group(
                state_buf[g][rows_of], state_buf[3 + g][rows_of], state_buf[6 + g][rows_of], total[where], factor
            )
            weights[s, z, where] = new[0].astype(jnp.bfloat16)
            for i in range(3):
                new_states[3 * i + g][rows_of] = new[i]

    for c in crossed:
        update(c)
        spread(z, c)
    for c in plain:
        update(c)
        both(0, c, start)
        spread(z, c)

    def pass_on(distance, c, among, act):
        for side in range(2):
            section = z + distance * (2 * side - 1)
            there = section >= 0 if side == 0 else section <= last
            onward = z < last if side == 0 else z > 0

            @pl.when(there)
            def _():
                for j in among:
                    if act is start:
                        gz_copy(1 - side, j, section, c).wait_recv()

                    @pl.when(onward)
                    def _():
                        act(gz_copy(side, j, section, c))

                if c in plain:
                    for j in others:
                        act(gx_copy(j, s, section, c))

    def cross(distance):
        for c in crossed:
            if distance:
                pass_on(distance, c, planes, start)
            else:
                both(0, c, start)
                for j in others:
                    gx_copy(j, shard_at(shards - j), z, c).wait_recv()
                for j in others:
                    both(j, c, start)

    for distance in range(1, sections):
        for c in plain:
            pass_on(distance, c, [0], start)
        cross(distance - 1)
    cross(last)

    for copy in tail:
        copy.wait_send()
    for c in crossed:
        for j in others:
            gx_copy(j, s, z, c).wait_send()
        for j in planes:
            both(j, c, finished)
        for distance in range(1, sections):
            pass_on(distance, c, planes, finished)
    for c in plain:
        both(0, c, finished)
        for j in others:
            gx_copy(j, s, z, c).wait_send()
        for distance in range(1, sections):
            pass_on(distance, c, [0], finished)
    for k in range(sections):
        for c in plain:
            for j in others:
                gx_copy(j, shard_at(shards - j), k, c).wait_recv()


def finish(rows, *refs):
    sources, targets, sem = refs[:10], refs[10:22], refs[22]
    copies = []
    for g in range(3):
        start = sum(rows[:g])
        copies.append((sources[9].at[:, :, start : start + rows[g]], targets[9 + g]))
    copies += list(zip(sources[:9], targets[:9]))
    copies = [
        pltpu.make_async_copy(source, target, sem.at[i]) for i, (source, target) in enumerate(copies)
    ]
    for copy in copies:
        copy.start()
    for copy in copies:
        copy.wait()


def on_device(*arguments):
    shards, sections, tensors = (lax.axis_size(a) for a in ("shard", "section", "tensor"))
    grads, states = arguments[:3], arguments[3:]
    batches, _, width = grads[0].shape
    rows = [states[g].shape[0] for g in range(3)]
    height = sum(rows)
    entries = sum(gradient.shape[1] * width * tensors for gradient in grads)
    ceiling = clip_rms * math.sqrt(entries)
    grads = [
        gradient.reshape(batches, shards, sections, rows[g], width) for g, gradient in enumerate(grads)
    ]
    count = len(cut(rows)[0])
    devices = shards * sections * tensors
    messages = devices - 1 if devices <= DIRECT_DEVICES else shards * sections + tensors - 2
    dma = pltpu.SemaphoreType.DMA
    scratch = (
        [pltpu.VMEM(gradient.shape, jnp.bfloat16) for gradient in grads]
        + [pltpu.VMEM(state.shape, jnp.float32) for state in states]
        + [
            pltpu.VMEM((shards - 1, sections, height, width), WIRE),
            pltpu.VMEM((shards - 1, sections, height, width), WIRE),
            pltpu.VMEM((shards, sections - 1, height, width), WIRE),
            pltpu.VMEM((2, shards, sections, height, width), WIRE),
            pltpu.VMEM((shards - 1, height, width), WIRE),
            pltpu.VMEM((shards - 1, height, width), WIRE),
            pltpu.VMEM((height, width), jnp.float32),
            pltpu.VMEM((1, 128), jnp.float32),
            pltpu.VMEM((messages, 1, 128), jnp.float32),
            pltpu.VMEM((1, 128), jnp.float32),
            dma((shards, sections, 3)),
            dma((9,)),
            dma((shards - 1, sections, count)),
            dma((shards - 1, sections, count)),
            dma((shards, sections - 1, count)),
            dma((2, shards, sections, count)),
            dma((shards - 1, count)),
            dma((shards - 1, count)),
            dma((messages,)),
            dma((messages,)),
            dma((shards - 1, sections, count)),
            dma((shards - 1, sections, count)),
            dma((2, shards, sections, count)),
            dma((shards, sections, count)),
        ]
    )
    results = pl.pallas_call(
        functools.partial(kernel, (shards, sections, tensors), rows, batches, ceiling),
        out_shape=[pltpu.VMEM(state.shape, jnp.float32) for state in states]
        + [pltpu.VMEM((shards, sections, height, width), jnp.bfloat16)],
        in_specs=[pl.BlockSpec(memory_space=pltpu.HBM)] * 12,
        out_specs=[pl.BlockSpec(memory_space=pltpu.VMEM)] * 10,
        scratch_shapes=scratch,
        compiler_params=pltpu.CompilerParams(
            collective_id=0, has_side_effects=True, vmem_limit_bytes=VMEM_LIMIT
        ),
    )(*grads, *states)
    full = [
        jax.ShapeDtypeStruct((shards, sections, rows[g], width), jnp.bfloat16) for g in range(3)
    ]
    finished = pl.pallas_call(
        functools.partial(finish, rows),
        out_shape=[jax.ShapeDtypeStruct(state.shape, jnp.float32) for state in states] + full,
        in_specs=[pl.BlockSpec(memory_space=pl.ANY)] * 10,
        out_specs=[pl.BlockSpec(memory_space=pltpu.HBM)] * 12,
        scratch_shapes=[dma((12,))],
        compiler_params=pltpu.CompilerParams(vmem_limit_bytes=4 * 1024 * 1024),
    )(*results)
    weights = [part.reshape(-1, width) for part in finished[9:]]
    return (*finished[:9], *weights)


def solution(mesh):
    grad = P(("shard", "section"), None, "tensor")
    state = P(("shard", "section"), "tensor")
    return jax.shard_map(
        on_device,
        mesh=mesh,
        in_specs=(grad,) * 3 + (state,) * 9,
        out_specs=(state,) * 9 + (P(None, "tensor"),) * 3,
        check_vma=False,
    )
```

```python
import functools
import math

import jax
import jax.numpy as jnp
from jax import lax
from jax.experimental import pallas as pl
from jax.experimental.pallas import tpu as pltpu
from jax.sharding import PartitionSpec as P

STEP = 10

beta_one = 0.9
beta_two = 0.95
adam_eps = 1e-08
learn_rate = 0.05
weight_decay = 0.1
clip_rms = 0.5

WIRE = jnp.bfloat16
VMEM_LIMIT = 56 * 1024 * 1024
PIECE_ROWS = 32
CROSSED_ROWS = 32
DIRECT_DEVICES = 64
MESH = pl.DeviceIdType.MESH


def adamw_group(master, moment, second, summed, factor):
    clipped = factor * summed
    moment_new = beta_one * moment + (1.0 - beta_one) * clipped
    second_new = beta_two * second + (1.0 - beta_two) * clipped * clipped
    first_hat = moment_new / (1.0 - beta_one**STEP)
    second_hat = second_new / (1.0 - beta_two**STEP)
    master_new = master - learn_rate * (
        first_hat / (jnp.sqrt(second_hat) + adam_eps) + weight_decay * master
    )
    return (master_new, moment_new, second_new)


def cut(rows):
    height = sum(rows)
    if any(r % 16 for r in rows) or height <= 4 * PIECE_ROWS:
        return [(0, height)], None
    plain = height - CROSSED_ROWS
    pieces = [(first, min(PIECE_ROWS, plain - first)) for first in range(0, plain, PIECE_ROWS)]
    return pieces, (plain, CROSSED_ROWS)


def kernel(sizes, rows, batches, ceiling, *refs):
    shards, sections, tensors = sizes
    grads, states = refs[0:3], refs[3:12]
    new_states, weights = refs[12:14]
    (
        grad_buf, state_buf, x_out, x_in, z_out, z_in, k_out, k_in, total, norms, norm_mid,
        load_sem, state_sem, x_recv, z_recv, c_recv, k_recv, norm_recv,
        x_send, k_send, z_send, c_send, norm_send, gx_send, gk_send, gz_send, gc_send,
    ) = refs[14:]
    s, t, z = lax.axis_index("shard"), lax.axis_index("tensor"), lax.axis_index("section")
    last = sections - 1
    pieces, crossed = cut(rows)
    plain = pl.ds(0, pieces[-1][0] + pieces[-1][1])
    starts = [sum(rows[:g]) for g in range(3)]
    planes = range(shards)
    others = range(1, shards)

    def shard_at(j):
        return lax.rem(s + j, shards)

    def span(piece):
        return pl.ds(piece[0], piece[1])

    def remote(source, target, send, receive, device):
        return pltpu.make_async_remote_copy(
            src_ref=source,
            dst_ref=target,
            send_sem=send,
            recv_sem=receive,
            device_id=device,
            device_id_type=MESH,
        )

    lo, hi = jnp.int32(0), jnp.int32(last)
    order = []
    for _ in range(sections):
        high = hi - z > z - lo
        order.append(jnp.where(high, hi, lo))
        lo, hi = jnp.where(high, lo, lo + 1), jnp.where(high, hi - 1, hi)

    def load(j, k):
        for g in range(3):
            pltpu.make_async_copy(
                grads[g].at[:, shard_at(j), order[k]],
                grad_buf.at[:, j, k, pl.ds(starts[g], rows[g])],
                load_sem.at[j, k],
            ).start()

    def loaded(j, k):
        place = grad_buf.at[:, j, k]
        pltpu.make_async_copy(place, place, load_sem.at[j, k]).wait()

    for j in others:
        load(j, 0)

    barrier = pltpu.get_barrier_semaphore()
    for j in others:
        pl.semaphore_signal(barrier, inc=1, device_id={"shard": shard_at(j)}, device_id_type=MESH)
    for c in range(1, tensors):
        pl.semaphore_signal(barrier, inc=1, device_id={"tensor": lax.rem(t + c, tensors)}, device_id_type=MESH)

    @pl.when(z > 0)
    def _():
        pl.semaphore_signal(barrier, inc=1, device_id={"section": z - 1}, device_id_type=MESH)

    @pl.when(z < last)
    def _():
        pl.semaphore_signal(barrier, inc=1, device_id={"section": z + 1}, device_id_type=MESH)

    for k in range(1, sections):
        for j in others:
            load(j, k)
    for k in range(sections):
        load(0, k)
    for i in range(3):
        for g in range(3):
            pltpu.make_async_copy(
                states[3 * i + g], state_buf.at[i, pl.ds(starts[g], rows[g])], state_sem
            ).start()

    def partial(j, k, piece):
        value = grad_buf[0, j, k, span(piece)].astype(jnp.float32)
        for m in range(1, batches):
            value = value + grad_buf[m, j, k, span(piece)].astype(jnp.float32)
        return value

    def x_copy(j, k, c):
        return remote(
            x_out.at[j - 1, k, span(pieces[c])], x_in.at[j - 1, k, span(pieces[c])],
            x_send, x_recv.at[j - 1, k, c], {"shard": shard_at(j)},
        )

    for k in range(sections):
        for j in others:
            loaded(j, k)
            for c, piece in enumerate(pieces):
                x_out[j - 1, k, span(piece)] = partial(j, k, piece).astype(WIRE)
                if (j, k, c) == (1, 0, 0):
                    neighbours = jnp.where(z > 0, 1, 0) + jnp.where(z < last, 1, 0)
                    pl.semaphore_wait(barrier, shards - 1 + tensors - 1 + neighbours)
                x_copy(j, k, c).start()
    for k in range(sections):
        loaded(0, k)

    @pl.when(z == 0)
    def _():
        z_in[:, 0:sections] = jnp.zeros((shards, sections) + z_in.shape[2:], WIRE)

    @pl.when(z == last)
    def _():
        z_in[:, 0:last] = jnp.zeros((shards, last) + z_in.shape[2:], WIRE)
        z_in[:, sections] = jnp.zeros((shards,) + z_in.shape[2:], WIRE)

    def z_semaphore(j, slot, c):
        return c_recv.at[j, slot] if c is None else z_recv.at[slot, c]

    def z_wait(j, slot, c):
        piece = crossed if c is None else pieces[c]
        place = z_in.at[j, slot, span(piece)]
        remote(place, place, z_send, z_semaphore(j, slot, c), {"section": z}).wait_recv()

    def z_copy(j, k, c):
        piece = crossed if c is None else pieces[c]
        up = jnp.where(order[k] > z, 1, 0)
        target = z + 2 * up - 1
        slot = jnp.where(jnp.logical_and(up == 0, target == order[k]), sections, order[k])
        return remote(
            z_out.at[j, k, span(piece)], z_in.at[j, slot, span(piece)],
            c_send if c is None else z_send, z_semaphore(j, slot, c), {"section": target},
        )

    def x_wait(k, c):
        for j in others:
            x_copy(j, k, c).wait_recv()

    inner = jnp.logical_and(z > 0, z < last)

    def z_step(j, k, c):
        piece = crossed if c is None else pieces[c]
        value = partial(j, k, piece)
        if c is not None:
            x_wait(k, c)
            for i in others:
                value = value + x_in[i - 1, k, span(piece)].astype(jnp.float32)

        @pl.when(inner)
        def _():
            z_wait(j, order[k], c)

        value = value + z_in[j, order[k], span(piece)].astype(jnp.float32)
        z_out[j, k, span(piece)] = value.astype(WIRE)
        z_copy(j, k, c).start()

    for k in range(last):
        if crossed:
            for j in planes:
                z_step(j, k, None)
        for c in range(len(pieces)):
            z_step(0, k, c)

    def arrived(j, c):
        piece = crossed if c is None else pieces[c]

        @pl.when(z > 0)
        def _():
            z_wait(j, z, c)

        @pl.when(z < last)
        def _():
            z_wait(j, sections, c)

        value = partial(j, last, piece)
        value = value + z_in[j, z, span(piece)].astype(jnp.float32)
        return value + z_in[j, sections, span(piece)].astype(jnp.float32)

    def k_copy(j):
        return remote(
            k_out.at[j - 1], k_in.at[j - 1], k_send.at[j - 1], k_recv.at[j - 1], {"shard": shard_at(j)}
        )

    if crossed:
        for j in others:
            k_out[j - 1] = arrived(j, None).astype(WIRE)
            k_copy(j).start()

    squares = jnp.zeros((1, total.shape[1]), jnp.float32)
    for c in [*range(len(pieces)), None]:
        piece = crossed if c is None else pieces[c]
        if piece is None:
            continue
        value = arrived(0, c)
        if c is None:
            for j in others:
                k_copy(j).wait_recv()
                value = value + k_in[j - 1].astype(jnp.float32)
        else:
            x_wait(last, c)
            for j in others:
                value = value + x_in[j - 1, last, span(piece)].astype(jnp.float32)
        total[span(piece)] = value
        squares = squares + jnp.sum(value * value, axis=0, keepdims=True)

    value = sum(squares[:, c : c + 128] for c in range(0, squares.shape[1], 128))

    def exchange(number, source, slots, mine, value, devices):
        source[mine] = value
        count = len(devices)
        for device in devices:
            remote(source.at[mine], slots.at[mine], norm_send.at[number], norm_recv.at[number], device).start()
        return remote(
            slots.at[pl.ds(0, count)], slots.at[pl.ds(0, count)],
            norm_send.at[number], norm_recv.at[number], {"section": z},
        )

    near = [(j, k) for k in range(sections) for j in planes]
    if shards * sections * tensors <= DIRECT_DEVICES:
        copy = exchange(
            0, norms, norms, (s * tensors + t) * sections + z, value,
            [
                {"shard": shard_at(j), "tensor": lax.rem(t + c, tensors), "section": order[k]}
                for j, k in near for c in range(tensors) if (j, k, c) != (0, last, 0)
            ],
        )
        messages = [copy]
    else:
        copy = exchange(
            0, norms, norms, s * sections + z, value,
            [{"shard": shard_at(j), "section": order[k]} for j, k in near if (j, k) != (0, last)],
        )
        messages = [copy]
    place = state_buf
    pltpu.make_async_copy(place, place, state_sem).wait()
    messages[0].wait_recv()
    value = jnp.sum(norms[...], axis=0)
    if shards * sections * tensors > DIRECT_DEVICES:
        copy = exchange(
            1, norm_mid, norm_mid, t, value, [{"tensor": lax.rem(t + c, tensors)} for c in range(1, tensors)]
        )
        messages.append(copy)
        copy.wait_recv()
        value = jnp.sum(norm_mid[...], axis=0)
    norm = jnp.sqrt(jnp.sum(value, axis=1, keepdims=True))
    factor = ceiling / jnp.maximum(norm, ceiling)

    def gx_copy(j, plane, section, c):
        piece = crossed if c is None else pieces[c]
        place = weights.at[plane, section, span(piece)]
        receive = k_recv.at[j - 1] if c is None else x_recv.at[j - 1, section, c]
        send = (gk_send if c is None else gx_send).at[j - 1]
        return remote(place, place, send, receive, {"shard": shard_at(j)})

    def gz_copy(side, j, section, c):
        piece = crossed if c is None else pieces[c]
        place = weights.at[shard_at(j), section, span(piece)]
        send = (gc_send if c is None else gz_send).at[side, section]
        return remote(place, place, send, z_semaphore(j, section, c), {"section": z + 1 - 2 * side})

    def gz_both(j, c):
        @pl.when(z < last)
        def _():
            gz_copy(0, j, z, c).start()

        @pl.when(z > 0)
        def _():
            gz_copy(1, j, z, c).start()

    def update(piece):
        new = adamw_group(
            state_buf[0, span(piece)], state_buf[1, span(piece)], state_buf[2, span(piece)],
            total[span(piece)], factor,
        )
        weights[s, z, span(piece)] = new[0].astype(jnp.bfloat16)
        for i in range(3):
            new_states[i, span(piece)] = new[i]

    if crossed:
        update(crossed)
        for j in others:
            gx_copy(j, s, z, None).start()
    for c, piece in enumerate(pieces):
        update(piece)
        gz_both(0, c)
        for j in others:
            gx_copy(j, s, z, c).start()

    def origin(side, distance):
        section = z + distance * (2 * side - 1)
        there = section >= 0 if side == 0 else section <= last
        onward = z < last if side == 0 else z > 0
        return section, there, onward

    def pass_on(side, distance, j, c):
        section, there, onward = origin(side, distance)

        @pl.when(there)
        def _():
            gz_copy(1 - side, j, section, c).wait_recv()

            @pl.when(onward)
            def _():
                gz_copy(side, j, section, c).start()

            if c is not None:
                for i in others:
                    gx_copy(i, s, section, c).start()

    def cross(distance):
        for j in planes:
            if distance:
                for side in range(2):
                    pass_on(side, distance, j, None)
            else:
                if j:
                    gx_copy(j, shard_at(shards - j), z, None).wait_recv()
                gz_both(shards - j if j else 0, None)

    place = x_out.at[:, :, plain]
    remote(place, place, x_send, k_recv.at[0], {"section": z}).wait_send()
    place = z_out.at[0, :, plain]
    remote(place, place, z_send, k_recv.at[0], {"section": z}).wait_send()
    if crossed:
        place = z_out.at[:, :, span(crossed)]
        remote(place, place, c_send, k_recv.at[0], {"section": z}).wait_send()
        for j in others:
            k_copy(j).wait_send()
    for copy in messages:
        copy.wait_send()

    for distance in range(1, sections):
        for c in range(len(pieces)):
            for side in range(2):
                pass_on(side, distance, 0, c)
        if crossed:
            cross(distance - 1)
    if crossed:
        cross(last)

    def sent(side, section):
        place = weights.at[s, section, plain]
        remote(place, place, gz_send.at[side, section], k_recv.at[0], {"section": z}).wait_send()
        if crossed:
            place = weights.at[:, section, span(crossed)]
            remote(place, place, gc_send.at[side, section], k_recv.at[0], {"section": z}).wait_send()

    for side in range(2):
        for distance in range(sections):
            section, there, onward = origin(side, distance)

            @pl.when(jnp.logical_and(there, onward))
            def _():
                sent(side, section)

    for j in others:
        place = weights.at[s, :, plain]
        remote(place, place, gx_send.at[j - 1], k_recv.at[0], {"section": z}).wait_send()
        if crossed:
            gx_copy(j, s, z, None).wait_send()
    for section in range(sections):
        for c in range(len(pieces)):
            for j in others:
                gx_copy(j, shard_at(shards - j), section, c).wait_recv()


def finish(rows, *refs):
    states, weights, targets, sem = refs[0], refs[1], refs[2:14], refs[14]
    copies = []
    for g in range(3):
        part = pl.ds(sum(rows[:g]), rows[g])
        copies.append((weights.at[:, :, part], targets[9 + g]))
        copies += [(states.at[i, part], targets[3 * i + g]) for i in range(3)]
    copies = [
        pltpu.make_async_copy(source, target, sem.at[i]) for i, (source, target) in enumerate(copies)
    ]
    for copy in copies:
        copy.start()
    for copy in copies:
        copy.wait()


def on_device(*arguments):
    shards, sections, tensors = (lax.axis_size(a) for a in ("shard", "section", "tensor"))
    grads, states = arguments[:3], arguments[3:]
    batches, _, width = grads[0].shape
    rows = [states[g].shape[0] for g in range(3)]
    height = sum(rows)
    entries = sum(gradient.shape[1] * width * tensors for gradient in grads)
    ceiling = clip_rms * math.sqrt(entries)
    grads = [
        gradient.reshape(batches, shards, sections, rows[g], width) for g, gradient in enumerate(grads)
    ]
    pieces, crossed = cut(rows)
    count = len(pieces)
    across = crossed[1] if crossed else 16
    devices = shards * sections * tensors
    dma = pltpu.SemaphoreType.DMA
    scratch = [
        pltpu.VMEM((batches, shards, sections, height, width), jnp.bfloat16),
        pltpu.VMEM((3, height, width), jnp.float32),
        pltpu.VMEM((shards - 1, sections, height, width), WIRE),
        pltpu.VMEM((shards - 1, sections, height, width), WIRE),
        pltpu.VMEM((shards, sections - 1, height, width), WIRE),
        pltpu.VMEM((shards, sections + 1, height, width), WIRE),
        pltpu.VMEM((shards - 1, across, width), WIRE),
        pltpu.VMEM((shards - 1, across, width), WIRE),
        pltpu.VMEM((height, width), jnp.float32),
        pltpu.VMEM((devices if devices <= DIRECT_DEVICES else shards * sections, 1, 128), jnp.float32),
        pltpu.VMEM((tensors, 1, 128), jnp.float32),
        dma((shards, sections)),
        dma,
        dma((shards - 1, sections, count)),
        dma((sections + 1, count)),
        dma((shards, sections + 1)),
        dma((shards - 1,)),
        dma((2,)),
        dma,
        dma((shards - 1,)),
        dma,
        dma,
        dma((2,)),
        dma((shards - 1,)),
        dma((shards - 1,)),
        dma((2, sections)),
        dma((2, sections)),
    ]
    results = pl.pallas_call(
        functools.partial(kernel, (shards, sections, tensors), rows, batches, ceiling),
        out_shape=[
            pltpu.VMEM((3, height, width), jnp.float32),
            pltpu.VMEM((shards, sections, height, width), jnp.bfloat16),
        ],
        in_specs=[pl.BlockSpec(memory_space=pltpu.HBM)] * 12,
        out_specs=[pl.BlockSpec(memory_space=pltpu.VMEM)] * 2,
        scratch_shapes=scratch,
        compiler_params=pltpu.CompilerParams(
            collective_id=0, has_side_effects=True, vmem_limit_bytes=VMEM_LIMIT
        ),
    )(*grads, *states)
    full = [
        jax.ShapeDtypeStruct((shards, sections, rows[g], width), jnp.bfloat16) for g in range(3)
    ]
    finished = pl.pallas_call(
        functools.partial(finish, rows),
        out_shape=[jax.ShapeDtypeStruct(state.shape, jnp.float32) for state in states] + full,
        in_specs=[pl.BlockSpec(memory_space=pl.ANY)] * 2,
        out_specs=[pl.BlockSpec(memory_space=pltpu.HBM)] * 12,
        scratch_shapes=[dma((12,))],
        compiler_params=pltpu.CompilerParams(vmem_limit_bytes=4 * 1024 * 1024),
    )(*results)
    weights = [part.reshape(-1, width) for part in finished[9:]]
    return (*finished[:9], *weights)


def solution(mesh):
    grad = P(("shard", "section"), None, "tensor")
    state = P(("shard", "section"), "tensor")
    return jax.shard_map(
        on_device,
        mesh=mesh,
        in_specs=(grad,) * 3 + (state,) * 9,
        out_specs=(state,) * 9 + (P(None, "tensor"),) * 3,
        check_vma=False,
    )
```

```python
import functools
import math

import jax
import jax.numpy as jnp
from jax import lax
from jax.experimental import pallas as pl
from jax.experimental.pallas import tpu as pltpu
from jax.sharding import PartitionSpec as P

STEP = 10

beta_one = 0.9
beta_two = 0.95
adam_eps = 1e-08
learn_rate = 0.05
weight_decay = 0.1
clip_rms = 0.5

WIRE = jnp.bfloat16
VMEM_LIMIT = 56 * 1024 * 1024
PIECE_ROWS = 32
CROSSED_ROWS = 32
DIRECT_DEVICES = 64
MESH = pl.DeviceIdType.MESH


def adamw_group(master, moment, second, summed, factor):
    clipped = factor * summed
    moment_new = beta_one * moment + (1.0 - beta_one) * clipped
    second_new = beta_two * second + (1.0 - beta_two) * clipped * clipped
    first_hat = moment_new / (1.0 - beta_one**STEP)
    second_hat = second_new / (1.0 - beta_two**STEP)
    master_new = master - learn_rate * (
        first_hat / (jnp.sqrt(second_hat) + adam_eps) + weight_decay * master
    )
    return (master_new, moment_new, second_new)


def cut(rows):
    height = sum(rows)
    if any(r % 16 for r in rows) or height <= 4 * PIECE_ROWS:
        return [(0, height)], None
    plain = height - CROSSED_ROWS
    pieces = [(first, min(PIECE_ROWS, plain - first)) for first in range(0, plain, PIECE_ROWS)]
    return pieces, (plain, CROSSED_ROWS)


def kernel(sizes, rows, batches, ceiling, *refs):
    shards, sections, tensors = sizes
    grads, states = refs[0:3], refs[3:12]
    new_states, weights = refs[12:14]
    (
        grad_buf, state_buf, x_out, x_in, z_out, z_in, k_out, k_in, total, norms, norm_mid,
        load_sem, state_sem, x_recv, z_recv, c_recv, k_recv, norm_recv,
        x_send, k_send, z_send, c_send, norm_send, gx_send, gk_send, gz_send, gc_send,
    ) = refs[14:]
    s, t, z = lax.axis_index("shard"), lax.axis_index("tensor"), lax.axis_index("section")
    last = sections - 1
    pieces, crossed = cut(rows)
    plain = pl.ds(0, pieces[-1][0] + pieces[-1][1])
    starts = [sum(rows[:g]) for g in range(3)]
    planes = range(shards)
    others = range(1, shards)

    def shard_at(j):
        return lax.rem(s + j, shards)

    def span(piece):
        return pl.ds(piece[0], piece[1])

    def remote(source, target, send, receive, device):
        return pltpu.make_async_remote_copy(
            src_ref=source,
            dst_ref=target,
            send_sem=send,
            recv_sem=receive,
            device_id=device,
            device_id_type=MESH,
        )

    lo, hi = jnp.int32(0), jnp.int32(last)
    order = []
    for _ in range(sections):
        high = jnp.where(2 * z > last, hi - z >= z - lo, hi - z > z - lo)
        high = jnp.logical_and(high, hi > z)
        order.append(jnp.where(high, hi, lo))
        lo, hi = jnp.where(high, lo, lo + 1), jnp.where(high, hi - 1, hi)

    def load(j, k):
        for g in range(3):
            pltpu.make_async_copy(
                grads[g].at[:, shard_at(j), order[k]],
                grad_buf.at[:, j, k, pl.ds(starts[g], rows[g])],
                load_sem.at[j, k],
            ).start()

    def loaded(j, k):
        place = grad_buf.at[:, j, k]
        pltpu.make_async_copy(place, place, load_sem.at[j, k]).wait()

    for j in others:
        load(j, 0)

    barrier = pltpu.get_barrier_semaphore()
    for j in others:
        pl.semaphore_signal(barrier, inc=1, device_id={"shard": shard_at(j)}, device_id_type=MESH)
    for c in range(1, tensors):
        pl.semaphore_signal(barrier, inc=1, device_id={"tensor": lax.rem(t + c, tensors)}, device_id_type=MESH)

    @pl.when(z > 0)
    def _():
        pl.semaphore_signal(barrier, inc=1, device_id={"section": z - 1}, device_id_type=MESH)

    @pl.when(z < last)
    def _():
        pl.semaphore_signal(barrier, inc=1, device_id={"section": z + 1}, device_id_type=MESH)

    for k in range(1, sections):
        for j in others:
            load(j, k)
    for k in range(sections):
        load(0, k)
    for i in range(3):
        for g in range(3):
            pltpu.make_async_copy(
                states[3 * i + g], state_buf.at[i, pl.ds(starts[g], rows[g])], state_sem
            ).start()

    def partial(j, k, piece):
        value = grad_buf[0, j, k, span(piece)].astype(jnp.float32)
        for m in range(1, batches):
            value = value + grad_buf[m, j, k, span(piece)].astype(jnp.float32)
        return value

    def x_copy(j, k, c):
        return remote(
            x_out.at[j - 1, k, span(pieces[c])], x_in.at[j - 1, k, span(pieces[c])],
            x_send, x_recv.at[j - 1, k, c], {"shard": shard_at(j)},
        )

    for k in range(sections):
        for j in others:
            loaded(j, k)
            for c, piece in enumerate(pieces):
                x_out[j - 1, k, span(piece)] = partial(j, k, piece).astype(WIRE)
                if (j, k, c) == (1, 0, 0):
                    neighbours = jnp.where(z > 0, 1, 0) + jnp.where(z < last, 1, 0)
                    pl.semaphore_wait(barrier, shards - 1 + tensors - 1 + neighbours)
                x_copy(j, k, c).start()
    for k in range(sections):
        loaded(0, k)

    @pl.when(z == 0)
    def _():
        z_in[:, 0:sections] = jnp.zeros((shards, sections) + z_in.shape[2:], WIRE)

    @pl.when(z == last)
    def _():
        z_in[:, 0:last] = jnp.zeros((shards, last) + z_in.shape[2:], WIRE)
        z_in[:, sections] = jnp.zeros((shards,) + z_in.shape[2:], WIRE)

    def z_semaphore(j, slot, c):
        return c_recv.at[j, slot] if c is None else z_recv.at[slot, c]

    def z_wait(j, slot, c):
        piece = crossed if c is None else pieces[c]
        place = z_in.at[j, slot, span(piece)]
        remote(place, place, z_send, z_semaphore(j, slot, c), {"section": z}).wait_recv()

    def z_copy(j, k, c):
        piece = crossed if c is None else pieces[c]
        up = jnp.where(order[k] > z, 1, 0)
        target = z + 2 * up - 1
        slot = jnp.where(jnp.logical_and(up == 0, target == order[k]), sections, order[k])
        return remote(
            z_out.at[j, k, span(piece)], z_in.at[j, slot, span(piece)],
            c_send if c is None else z_send, z_semaphore(j, slot, c), {"section": target},
        )

    def x_wait(k, c):
        for j in others:
            x_copy(j, k, c).wait_recv()

    inner = jnp.logical_and(z > 0, z < last)

    def z_step(j, k, c):
        piece = crossed if c is None else pieces[c]
        value = partial(j, k, piece)
        if c is not None:
            x_wait(k, c)
            for i in others:
                value = value + x_in[i - 1, k, span(piece)].astype(jnp.float32)

        @pl.when(inner)
        def _():
            z_wait(j, order[k], c)

        value = value + z_in[j, order[k], span(piece)].astype(jnp.float32)
        z_out[j, k, span(piece)] = value.astype(WIRE)
        z_copy(j, k, c).start()

    def arrived(j, c):
        piece = crossed if c is None else pieces[c]

        @pl.when(z > 0)
        def _():
            z_wait(j, z, c)

        @pl.when(z < last)
        def _():
            z_wait(j, sections, c)

        value = partial(j, last, piece)
        value = value + z_in[j, z, span(piece)].astype(jnp.float32)
        return value + z_in[j, sections, span(piece)].astype(jnp.float32)

    def k_copy(j):
        return remote(
            k_out.at[j - 1], k_in.at[j - 1], k_send.at[j - 1], k_recv.at[j - 1], {"shard": shard_at(j)}
        )

    def cross_step(k):
        for j in planes:
            if k < last:
                z_step(j, k, None)
            elif j:
                k_out[j - 1] = arrived(j, None).astype(WIRE)
                k_copy(j).start()

    steps = [(k, c) for k in range(last) for c in range(len(pieces))]
    for k in reversed(range(sections)):
        steps.insert(max(0, k * len(pieces) - (2 if k == last else 1)), (k, None))
    for k, c in steps:
        if c is not None:
            z_step(0, k, c)
        elif crossed:
            cross_step(k)

    squares = jnp.zeros((1, total.shape[1]), jnp.float32)
    for c in [*range(len(pieces)), None]:
        piece = crossed if c is None else pieces[c]
        if piece is None:
            continue
        value = arrived(0, c)
        if c is None:
            for j in others:
                k_copy(j).wait_recv()
                value = value + k_in[j - 1].astype(jnp.float32)
        else:
            x_wait(last, c)
            for j in others:
                value = value + x_in[j - 1, last, span(piece)].astype(jnp.float32)
        total[span(piece)] = value
        squares = squares + jnp.sum(value * value, axis=0, keepdims=True)

    value = sum(squares[:, c : c + 128] for c in range(0, squares.shape[1], 128))

    def exchange(number, source, slots, mine, value, devices):
        source[mine] = value
        count = len(devices)
        for device in devices:
            remote(source.at[mine], slots.at[mine], norm_send.at[number], norm_recv.at[number], device).start()
        return remote(
            slots.at[pl.ds(0, count)], slots.at[pl.ds(0, count)],
            norm_send.at[number], norm_recv.at[number], {"section": z},
        )

    near = [(j, k) for k in range(sections) for j in planes]
    if shards * sections * tensors <= DIRECT_DEVICES:
        copy = exchange(
            0, norms, norms, (s * tensors + t) * sections + z, value,
            [
                {"shard": shard_at(j), "tensor": lax.rem(t + c, tensors), "section": order[k]}
                for j, k in near for c in range(tensors) if (j, k, c) != (0, last, 0)
            ],
        )
        messages = [copy]
    else:
        copy = exchange(
            0, norms, norms, s * sections + z, value,
            [{"shard": shard_at(j), "section": order[k]} for j, k in near if (j, k) != (0, last)],
        )
        messages = [copy]
    place = state_buf
    pltpu.make_async_copy(place, place, state_sem).wait()
    messages[0].wait_recv()
    value = jnp.sum(norms[...], axis=0)
    if shards * sections * tensors > DIRECT_DEVICES:
        copy = exchange(
            1, norm_mid, norm_mid, t, value, [{"tensor": lax.rem(t + c, tensors)} for c in range(1, tensors)]
        )
        messages.append(copy)
        copy.wait_recv()
        value = jnp.sum(norm_mid[...], axis=0)
    norm = jnp.sqrt(jnp.sum(value, axis=1, keepdims=True))
    factor = ceiling / jnp.maximum(norm, ceiling)

    def gx_copy(j, plane, section, c):
        piece = crossed if c is None else pieces[c]
        place = weights.at[plane, section, span(piece)]
        receive = k_recv.at[j - 1] if c is None else x_recv.at[j - 1, section, c]
        send = (gk_send if c is None else gx_send).at[j - 1]
        return remote(place, place, send, receive, {"shard": shard_at(j)})

    def gz_copy(side, j, section, c):
        piece = crossed if c is None else pieces[c]
        place = weights.at[shard_at(j), section, span(piece)]
        send = (gc_send if c is None else gz_send).at[side, section]
        return remote(place, place, send, z_semaphore(j, section, c), {"section": z + 1 - 2 * side})

    def gz_both(j, c):
        @pl.when(z < last)
        def _():
            gz_copy(0, j, z, c).start()

        @pl.when(z > 0)
        def _():
            gz_copy(1, j, z, c).start()

    def update(piece):
        new = adamw_group(
            state_buf[0, span(piece)], state_buf[1, span(piece)], state_buf[2, span(piece)],
            total[span(piece)], factor,
        )
        weights[s, z, span(piece)] = new[0].astype(jnp.bfloat16)
        for i in range(3):
            new_states[i, span(piece)] = new[i]

    if crossed:
        update(crossed)
        for j in others:
            gx_copy(j, s, z, None).start()
    for c, piece in enumerate(pieces):
        update(piece)
        gz_both(0, c)
        for j in others:
            gx_copy(j, s, z, c).start()

    def origin(side, distance):
        section = z + distance * (2 * side - 1)
        there = section >= 0 if side == 0 else section <= last
        onward = z < last if side == 0 else z > 0
        return section, there, onward

    def pass_on(side, distance, j, c):
        section, there, onward = origin(side, distance)

        @pl.when(there)
        def _():
            gz_copy(1 - side, j, section, c).wait_recv()

            @pl.when(onward)
            def _():
                gz_copy(side, j, section, c).start()

            if c is not None:
                for i in others:
                    gx_copy(i, s, section, c).start()

    def cross(distance):
        for j in planes:
            if distance:
                for side in range(2):
                    pass_on(side, distance, j, None)
            else:
                if j:
                    gx_copy(j, shard_at(shards - j), z, None).wait_recv()
                gz_both(shards - j if j else 0, None)

    place = x_out.at[:, :, plain]
    remote(place, place, x_send, k_recv.at[0], {"section": z}).wait_send()
    place = z_out.at[0, :, plain]
    remote(place, place, z_send, k_recv.at[0], {"section": z}).wait_send()
    if crossed:
        place = z_out.at[:, :, span(crossed)]
        remote(place, place, c_send, k_recv.at[0], {"section": z}).wait_send()
        for j in others:
            k_copy(j).wait_send()
    for copy in messages:
        copy.wait_send()

    for distance in range(1, sections):
        for c in range(len(pieces)):
            for side in range(2):
                pass_on(side, distance, 0, c)
        if crossed:
            cross(distance - 1)
    if crossed:
        cross(last)

    def sent(side, section):
        place = weights.at[s, section, plain]
        remote(place, place, gz_send.at[side, section], k_recv.at[0], {"section": z}).wait_send()
        if crossed:
            place = weights.at[:, section, span(crossed)]
            remote(place, place, gc_send.at[side, section], k_recv.at[0], {"section": z}).wait_send()

    for side in range(2):
        for distance in range(sections):
            section, there, onward = origin(side, distance)

            @pl.when(jnp.logical_and(there, onward))
            def _():
                sent(side, section)

    for j in others:
        place = weights.at[s, :, plain]
        remote(place, place, gx_send.at[j - 1], k_recv.at[0], {"section": z}).wait_send()
        if crossed:
            gx_copy(j, s, z, None).wait_send()
    for section in range(sections):
        for c in range(len(pieces)):
            for j in others:
                gx_copy(j, shard_at(shards - j), section, c).wait_recv()


def finish(rows, *refs):
    states, weights, targets, sem = refs[0], refs[1], refs[2:14], refs[14]
    copies = []
    for g in range(3):
        part = pl.ds(sum(rows[:g]), rows[g])
        copies.append((weights.at[:, :, part], targets[9 + g]))
        copies += [(states.at[i, part], targets[3 * i + g]) for i in range(3)]
    copies = [
        pltpu.make_async_copy(source, target, sem.at[i]) for i, (source, target) in enumerate(copies)
    ]
    for copy in copies:
        copy.start()
    for copy in copies:
        copy.wait()


def on_device(*arguments):
    shards, sections, tensors = (lax.axis_size(a) for a in ("shard", "section", "tensor"))
    grads, states = arguments[:3], arguments[3:]
    batches, _, width = grads[0].shape
    rows = [states[g].shape[0] for g in range(3)]
    height = sum(rows)
    entries = sum(gradient.shape[1] * width * tensors for gradient in grads)
    ceiling = clip_rms * math.sqrt(entries)
    grads = [
        gradient.reshape(batches, shards, sections, rows[g], width) for g, gradient in enumerate(grads)
    ]
    pieces, crossed = cut(rows)
    count = len(pieces)
    across = crossed[1] if crossed else 16
    devices = shards * sections * tensors
    dma = pltpu.SemaphoreType.DMA
    scratch = [
        pltpu.VMEM((batches, shards, sections, height, width), jnp.bfloat16),
        pltpu.VMEM((3, height, width), jnp.float32),
        pltpu.VMEM((shards - 1, sections, height, width), WIRE),
        pltpu.VMEM((shards - 1, sections, height, width), WIRE),
        pltpu.VMEM((shards, sections - 1, height, width), WIRE),
        pltpu.VMEM((shards, sections + 1, height, width), WIRE),
        pltpu.VMEM((shards - 1, across, width), WIRE),
        pltpu.VMEM((shards - 1, across, width), WIRE),
        pltpu.VMEM((height, width), jnp.float32),
        pltpu.VMEM((devices if devices <= DIRECT_DEVICES else shards * sections, 1, 128), jnp.float32),
        pltpu.VMEM((tensors, 1, 128), jnp.float32),
        dma((shards, sections)),
        dma,
        dma((shards - 1, sections, count)),
        dma((sections + 1, count)),
        dma((shards, sections + 1)),
        dma((shards - 1,)),
        dma((2,)),
        dma,
        dma((shards - 1,)),
        dma,
        dma,
        dma((2,)),
        dma((shards - 1,)),
        dma((shards - 1,)),
        dma((2, sections)),
        dma((2, sections)),
    ]
    results = pl.pallas_call(
        functools.partial(kernel, (shards, sections, tensors), rows, batches, ceiling),
        out_shape=[
            pltpu.VMEM((3, height, width), jnp.float32),
            pltpu.VMEM((shards, sections, height, width), jnp.bfloat16),
        ],
        in_specs=[pl.BlockSpec(memory_space=pltpu.HBM)] * 12,
        out_specs=[pl.BlockSpec(memory_space=pltpu.VMEM)] * 2,
        scratch_shapes=scratch,
        compiler_params=pltpu.CompilerParams(
            collective_id=0, has_side_effects=True, vmem_limit_bytes=VMEM_LIMIT
        ),
    )(*grads, *states)
    full = [
        jax.ShapeDtypeStruct((shards, sections, rows[g], width), jnp.bfloat16) for g in range(3)
    ]
    finished = pl.pallas_call(
        functools.partial(finish, rows),
        out_shape=[jax.ShapeDtypeStruct(state.shape, jnp.float32) for state in states] + full,
        in_specs=[pl.BlockSpec(memory_space=pl.ANY)] * 2,
        out_specs=[pl.BlockSpec(memory_space=pltpu.HBM)] * 12,
        scratch_shapes=[dma((12,))],
        compiler_params=pltpu.CompilerParams(vmem_limit_bytes=4 * 1024 * 1024),
    )(*results)
    weights = [part.reshape(-1, width) for part in finished[9:]]
    return (*finished[:9], *weights)


def solution(mesh):
    grad = P(("shard", "section"), None, "tensor")
    state = P(("shard", "section"), "tensor")
    return jax.shard_map(
        on_device,
        mesh=mesh,
        in_specs=(grad,) * 3 + (state,) * 9,
        out_specs=(state,) * 9 + (P(None, "tensor"),) * 3,
        check_vma=False,
    )
```

```python
import functools
import math

import jax
import jax.numpy as jnp
from jax import lax
from jax.experimental import pallas as pl
from jax.experimental.pallas import tpu as pltpu
from jax.sharding import PartitionSpec as P

STEP = 10

beta_one = 0.9
beta_two = 0.95
adam_eps = 1e-08
learn_rate = 0.05
weight_decay = 0.1
clip_rms = 0.5

WIRE = jnp.bfloat16
VMEM_LIMIT = 56 * 1024 * 1024
PIECE_ROWS = 32
CROSSED_ROWS = 32
DIRECT_DEVICES = 64
MESH = pl.DeviceIdType.MESH


def adamw_group(master, moment, second, summed, factor):
    clipped = factor * summed
    moment_new = beta_one * moment + (1.0 - beta_one) * clipped
    second_new = beta_two * second + (1.0 - beta_two) * clipped * clipped
    first_hat = moment_new / (1.0 - beta_one**STEP)
    second_hat = second_new / (1.0 - beta_two**STEP)
    master_new = master - learn_rate * (
        first_hat / (jnp.sqrt(second_hat) + adam_eps) + weight_decay * master
    )
    return (master_new, moment_new, second_new)


def cut(rows):
    height = sum(rows)
    if any(r % 16 for r in rows) or height <= 4 * PIECE_ROWS:
        return [(0, height)], None
    plain = height - CROSSED_ROWS
    pieces = [(first, min(PIECE_ROWS, plain - first)) for first in range(0, plain, PIECE_ROWS)]
    return pieces, (plain, CROSSED_ROWS)


def kernel(sizes, rows, batches, ceiling, *refs):
    shards, sections, tensors = sizes
    grads, states = refs[0:3], refs[3:12]
    new_states, weights = refs[12:14]
    (
        grad_buf, state_buf, x_out, x_in, z_out, z_in, k_out, k_in, total, norms, norm_mid,
        load_sem, state_sem, x_recv, z_recv, c_recv, k_recv, norm_recv,
        x_send, k_send, z_send, c_send, norm_send, gx_send, gk_send, gz_send, gc_send,
    ) = refs[14:]
    s, t, z = lax.axis_index("shard"), lax.axis_index("tensor"), lax.axis_index("section")
    last = sections - 1
    pieces, crossed = cut(rows)
    plain = pl.ds(0, pieces[-1][0] + pieces[-1][1])
    starts = [sum(rows[:g]) for g in range(3)]
    planes = range(shards)
    others = range(1, shards)

    def shard_at(j):
        return lax.rem(s + j, shards)

    def span(piece):
        return pl.ds(piece[0], piece[1])

    def remote(source, target, send, receive, device):
        return pltpu.make_async_remote_copy(
            src_ref=source,
            dst_ref=target,
            send_sem=send,
            recv_sem=receive,
            device_id=device,
            device_id_type=MESH,
        )

    lo, hi = jnp.int32(0), jnp.int32(last)
    order = []
    for _ in range(sections):
        high = jnp.where(2 * z > last, hi - z >= z - lo, hi - z > z - lo)
        high = jnp.logical_and(high, hi > z)
        order.append(jnp.where(high, hi, lo))
        lo, hi = jnp.where(high, lo, lo + 1), jnp.where(high, hi - 1, hi)

    def load(j, k):
        for g in range(3):
            pltpu.make_async_copy(
                grads[g].at[:, shard_at(j), order[k]],
                grad_buf.at[:, j, k, pl.ds(starts[g], rows[g])],
                load_sem.at[j, k],
            ).start()

    def loaded(j, k):
        place = grad_buf.at[:, j, k]
        pltpu.make_async_copy(place, place, load_sem.at[j, k]).wait()

    for j in others:
        load(j, 0)

    barrier = pltpu.get_barrier_semaphore()
    for j in others:
        pl.semaphore_signal(barrier, inc=1, device_id={"shard": shard_at(j)}, device_id_type=MESH)
    for c in range(1, tensors):
        pl.semaphore_signal(barrier, inc=1, device_id={"tensor": lax.rem(t + c, tensors)}, device_id_type=MESH)

    @pl.when(z > 0)
    def _():
        pl.semaphore_signal(barrier, inc=1, device_id={"section": z - 1}, device_id_type=MESH)

    @pl.when(z < last)
    def _():
        pl.semaphore_signal(barrier, inc=1, device_id={"section": z + 1}, device_id_type=MESH)

    for k in range(1, sections):
        for j in others:
            load(j, k)
    for k in range(sections):
        load(0, k)
    for i in range(3):
        for g in range(3):
            pltpu.make_async_copy(
                states[3 * i + g], state_buf.at[i, pl.ds(starts[g], rows[g])], state_sem
            ).start()

    def partial(j, k, piece):
        value = grad_buf[0, j, k, span(piece)].astype(jnp.float32)
        for m in range(1, batches):
            value = value + grad_buf[m, j, k, span(piece)].astype(jnp.float32)
        return value

    def x_copy(j, k, c):
        return remote(
            x_out.at[j - 1, k, span(pieces[c])], x_in.at[j - 1, k, span(pieces[c])],
            x_send, x_recv.at[j - 1, k, c], {"shard": shard_at(j)},
        )

    def z_semaphore(j, slot, c):
        return c_recv.at[j, slot] if c is None else z_recv.at[slot, c]

    def z_wait(j, slot, c):
        piece = crossed if c is None else pieces[c]
        place = z_in.at[j, slot, span(piece)]
        remote(place, place, z_send, z_semaphore(j, slot, c), {"section": z}).wait_recv()

    def z_copy(j, k, c):
        piece = crossed if c is None else pieces[c]
        up = jnp.where(order[k] > z, 1, 0)
        target = z + 2 * up - 1
        slot = jnp.where(jnp.logical_and(up == 0, target == order[k]), sections, order[k])
        return remote(
            z_out.at[j, k, span(piece)], z_in.at[j, slot, span(piece)],
            c_send if c is None else z_send, z_semaphore(j, slot, c), {"section": target},
        )

    def x_wait(k, c):
        for j in others:
            x_copy(j, k, c).wait_recv()

    inner = jnp.logical_and(z > 0, z < last)

    def arrived(j, c):
        piece = crossed if c is None else pieces[c]

        @pl.when(z > 0)
        def _():
            z_wait(j, z, c)

        @pl.when(z < last)
        def _():
            z_wait(j, sections, c)

        value = partial(j, last, piece)
        value = value + z_in[j, z, span(piece)].astype(jnp.float32)
        return value + z_in[j, sections, span(piece)].astype(jnp.float32)

    def k_copy(j):
        return remote(
            k_out.at[j - 1], k_in.at[j - 1], k_send.at[j - 1], k_recv.at[j - 1], {"shard": shard_at(j)}
        )

    def z_step(j, k, c, ready):
        piece = crossed if c is None else pieces[c]
        value = partial(j, k, piece)
        if c is not None:
            x_wait(k, c)
            for i in others:
                value = value + x_in[i - 1, k, span(piece)].astype(jnp.float32)
            pl.when(inner)(lambda: z_wait(j, order[k], c))
        elif ready:
            z_wait(j, order[k], c)
        if ready:
            value = value + z_in[j, order[k], span(piece)].astype(jnp.float32)
        z_out[j, k, span(piece)] = value.astype(WIRE)
        z_copy(j, k, c).start()

    def cross_step(k, ready):
        for j in planes:
            z_step(j, k, None, ready)

    for k in range(sections):
        for j in others:
            loaded(j, k)
            for c, piece in enumerate(pieces):
                x_out[j - 1, k, span(piece)] = partial(j, k, piece).astype(WIRE)
                if (j, k, c) == (1, 0, 0):
                    neighbours = jnp.where(z > 0, 1, 0) + jnp.where(z < last, 1, 0)
                    pl.semaphore_wait(barrier, shards - 1 + tensors - 1 + neighbours)
                x_copy(j, k, c).start()
        loaded(0, k)
        if crossed and k < last:
            pl.when(jnp.logical_not(inner))(lambda: cross_step(k, False))

    def clear(slots, own):
        for slot in slots:
            z_in[0, slot] = jnp.zeros(z_in.shape[2:], WIRE)
        if crossed:
            for j in others:
                z_in[j, own, span(crossed)] = jnp.zeros((crossed[1], z_in.shape[3]), WIRE)

    pl.when(z == 0)(lambda: clear([*range(sections)], 0))
    pl.when(z == last)(lambda: clear([*range(last), sections], sections))

    steps = [(k, c) for k in range(last) for c in range(len(pieces))]
    if crossed:
        for k in reversed(range(last)):
            steps.insert(2 * k * len(pieces) // 3, (k, None))
        steps.insert(len(steps) - 2, (last, None))
    for k, c in steps:
        if c is not None:
            z_step(0, k, c, True)
        elif k < last:
            pl.when(inner)(lambda: cross_step(k, True))
        else:
            for j in others:
                k_out[j - 1] = arrived(j, None).astype(WIRE)
                k_copy(j).start()

    squares = jnp.zeros((1, total.shape[1]), jnp.float32)
    for c in [*range(len(pieces)), None]:
        piece = crossed if c is None else pieces[c]
        if piece is None:
            continue
        value = arrived(0, c)
        if c is None:
            for j in others:
                k_copy(j).wait_recv()
                value = value + k_in[j - 1].astype(jnp.float32)
        else:
            x_wait(last, c)
            for j in others:
                value = value + x_in[j - 1, last, span(piece)].astype(jnp.float32)
        total[span(piece)] = value
        squares = squares + jnp.sum(value * value, axis=0, keepdims=True)

    value = sum(squares[:, c : c + 128] for c in range(0, squares.shape[1], 128))

    def exchange(number, source, slots, mine, value, devices):
        source[mine] = value
        count = len(devices)
        for device in devices:
            remote(source.at[mine], slots.at[mine], norm_send.at[number], norm_recv.at[number], device).start()
        return remote(
            slots.at[pl.ds(0, count)], slots.at[pl.ds(0, count)],
            norm_send.at[number], norm_recv.at[number], {"section": z},
        )

    near = [(j, k) for k in range(sections) for j in planes]
    if shards * sections * tensors <= DIRECT_DEVICES:
        copy = exchange(
            0, norms, norms, (s * tensors + t) * sections + z, value,
            [
                {"shard": shard_at(j), "tensor": lax.rem(t + c, tensors), "section": order[k]}
                for j, k in reversed(near) for c in range(tensors) if (j, k, c) != (0, last, 0)
            ],
        )
        messages = [copy]
    else:
        copy = exchange(
            0, norms, norms, s * sections + z, value,
            [{"shard": shard_at(j), "section": order[k]} for j, k in near if (j, k) != (0, last)],
        )
        messages = [copy]
    place = state_buf
    pltpu.make_async_copy(place, place, state_sem).wait()
    messages[0].wait_recv()
    value = jnp.sum(norms[...], axis=0)
    if shards * sections * tensors > DIRECT_DEVICES:
        copy = exchange(
            1, norm_mid, norm_mid, t, value, [{"tensor": lax.rem(t + c, tensors)} for c in range(1, tensors)]
        )
        messages.append(copy)
        copy.wait_recv()
        value = jnp.sum(norm_mid[...], axis=0)
    norm = jnp.sqrt(jnp.sum(value, axis=1, keepdims=True))
    factor = ceiling / jnp.maximum(norm, ceiling)

    def gx_copy(j, plane, section, c):
        piece = crossed if c is None else pieces[c]
        place = weights.at[plane, section, span(piece)]
        receive = k_recv.at[j - 1] if c is None else x_recv.at[j - 1, section, c]
        send = (gk_send if c is None else gx_send).at[j - 1]
        return remote(place, place, send, receive, {"shard": shard_at(j)})

    def gz_copy(side, j, section, c):
        piece = crossed if c is None else pieces[c]
        place = weights.at[shard_at(j), section, span(piece)]
        send = (gc_send if c is None else gz_send).at[side, section]
        return remote(place, place, send, z_semaphore(j, section, c), {"section": z + 1 - 2 * side})

    def gz_both(j, c):
        @pl.when(z < last)
        def _():
            gz_copy(0, j, z, c).start()

        @pl.when(z > 0)
        def _():
            gz_copy(1, j, z, c).start()

    def update(piece):
        new = adamw_group(
            state_buf[0, span(piece)], state_buf[1, span(piece)], state_buf[2, span(piece)],
            total[span(piece)], factor,
        )
        weights[s, z, span(piece)] = new[0].astype(jnp.bfloat16)
        for i in range(3):
            new_states[i, span(piece)] = new[i]

    for c, piece in enumerate(pieces):
        update(piece)
        gz_both(0, c)
        for j in others:
            gx_copy(j, s, z, c).start()
        if crossed and c == 0:
            update(crossed)
            for j in others:
                gx_copy(j, s, z, None).start()

    def origin(side, distance):
        section = z + distance * (2 * side - 1)
        there = section >= 0 if side == 0 else section <= last
        onward = z < last if side == 0 else z > 0
        return section, there, onward

    def pass_on(side, distance, j, c):
        section, there, onward = origin(side, distance)

        @pl.when(there)
        def _():
            gz_copy(1 - side, j, section, c).wait_recv()

            @pl.when(onward)
            def _():
                gz_copy(side, j, section, c).start()

            if c is not None:
                for i in others:
                    gx_copy(i, s, section, c).start()

    def cross(distance):
        for j in planes:
            if distance:
                for side in range(2):
                    pass_on(side, distance, j, None)
            else:
                if j:
                    gx_copy(j, shard_at(shards - j), z, None).wait_recv()
                gz_both(shards - j if j else 0, None)

    place = x_out.at[:, :, plain]
    remote(place, place, x_send, k_recv.at[0], {"section": z}).wait_send()
    place = z_out.at[0, :, plain]
    remote(place, place, z_send, k_recv.at[0], {"section": z}).wait_send()
    if crossed:
        place = z_out.at[:, :, span(crossed)]
        remote(place, place, c_send, k_recv.at[0], {"section": z}).wait_send()
        for j in others:
            k_copy(j).wait_send()
    for copy in messages:
        copy.wait_send()

    for distance in range(1, sections):
        for c in range(len(pieces)):
            for side in range(2):
                pass_on(side, distance, 0, c)
        if crossed:
            cross(distance - 1)
    if crossed:
        cross(last)

    def sent(side, section):
        place = weights.at[s, section, plain]
        remote(place, place, gz_send.at[side, section], k_recv.at[0], {"section": z}).wait_send()
        if crossed:
            place = weights.at[:, section, span(crossed)]
            remote(place, place, gc_send.at[side, section], k_recv.at[0], {"section": z}).wait_send()

    for side in range(2):
        for distance in range(sections):
            section, there, onward = origin(side, distance)

            @pl.when(jnp.logical_and(there, onward))
            def _():
                sent(side, section)

    for j in others:
        place = weights.at[s, :, plain]
        remote(place, place, gx_send.at[j - 1], k_recv.at[0], {"section": z}).wait_send()
        if crossed:
            gx_copy(j, s, z, None).wait_send()
    for section in range(sections):
        for c in range(len(pieces)):
            for j in others:
                gx_copy(j, shard_at(shards - j), section, c).wait_recv()


def finish(rows, *refs):
    states, weights, targets, sem = refs[0], refs[1], refs[2:14], refs[14]
    copies = []
    for g in range(3):
        part = pl.ds(sum(rows[:g]), rows[g])
        copies += [(states.at[i, part], targets[3 * i + g]) for i in range(3)]
    for g in range(3):
        copies.append((weights.at[:, :, pl.ds(sum(rows[:g]), rows[g])], targets[9 + g]))
    copies = [
        pltpu.make_async_copy(source, target, sem.at[i]) for i, (source, target) in enumerate(copies)
    ]
    for copy in copies:
        copy.start()
    for copy in copies:
        copy.wait()


def on_device(*arguments):
    shards, sections, tensors = (lax.axis_size(a) for a in ("shard", "section", "tensor"))
    grads, states = arguments[:3], arguments[3:]
    batches, _, width = grads[0].shape
    rows = [states[g].shape[0] for g in range(3)]
    height = sum(rows)
    entries = sum(gradient.shape[1] * width * tensors for gradient in grads)
    ceiling = clip_rms * math.sqrt(entries)
    grads = [
        gradient.reshape(batches, shards, sections, rows[g], width) for g, gradient in enumerate(grads)
    ]
    pieces, crossed = cut(rows)
    count = len(pieces)
    across = crossed[1] if crossed else 16
    devices = shards * sections * tensors
    dma = pltpu.SemaphoreType.DMA
    scratch = [
        pltpu.VMEM((batches, shards, sections, height, width), jnp.bfloat16),
        pltpu.VMEM((3, height, width), jnp.float32),
        pltpu.VMEM((shards - 1, sections, height, width), WIRE),
        pltpu.VMEM((shards - 1, sections, height, width), WIRE),
        pltpu.VMEM((shards, sections - 1, height, width), WIRE),
        pltpu.VMEM((shards, sections + 1, height, width), WIRE),
        pltpu.VMEM((shards - 1, across, width), WIRE),
        pltpu.VMEM((shards - 1, across, width), WIRE),
        pltpu.VMEM((height, width), jnp.float32),
        pltpu.VMEM((devices if devices <= DIRECT_DEVICES else shards * sections, 1, 128), jnp.float32),
        pltpu.VMEM((tensors, 1, 128), jnp.float32),
        dma((shards, sections)),
        dma,
        dma((shards - 1, sections, count)),
        dma((sections + 1, count)),
        dma((shards, sections + 1)),
        dma((shards - 1,)),
        dma((2,)),
        dma,
        dma((shards - 1,)),
        dma,
        dma,
        dma((2,)),
        dma((shards - 1,)),
        dma((shards - 1,)),
        dma((2, sections)),
        dma((2, sections)),
    ]
    results = pl.pallas_call(
        functools.partial(kernel, (shards, sections, tensors), rows, batches, ceiling),
        out_shape=[
            pltpu.VMEM((3, height, width), jnp.float32),
            pltpu.VMEM((shards, sections, height, width), jnp.bfloat16),
        ],
        in_specs=[pl.BlockSpec(memory_space=pltpu.HBM)] * 12,
        out_specs=[pl.BlockSpec(memory_space=pltpu.VMEM)] * 2,
        scratch_shapes=scratch,
        compiler_params=pltpu.CompilerParams(
            collective_id=0, has_side_effects=True, vmem_limit_bytes=VMEM_LIMIT
        ),
    )(*grads, *states)
    full = [
        jax.ShapeDtypeStruct((shards, sections, rows[g], width), jnp.bfloat16) for g in range(3)
    ]
    finished = pl.pallas_call(
        functools.partial(finish, rows),
        out_shape=[jax.ShapeDtypeStruct(state.shape, jnp.float32) for state in states] + full,
        in_specs=[pl.BlockSpec(memory_space=pl.ANY)] * 2,
        out_specs=[pl.BlockSpec(memory_space=pltpu.HBM)] * 12,
        scratch_shapes=[dma((12,))],
        compiler_params=pltpu.CompilerParams(vmem_limit_bytes=4 * 1024 * 1024),
    )(*results)
    weights = [part.reshape(-1, width) for part in finished[9:]]
    return (*finished[:9], *weights)


def solution(mesh):
    grad = P(("shard", "section"), None, "tensor")
    state = P(("shard", "section"), "tensor")
    return jax.shard_map(
        on_device,
        mesh=mesh,
        in_specs=(grad,) * 3 + (state,) * 9,
        out_specs=(state,) * 9 + (P(None, "tensor"),) * 3,
        check_vma=False,
    )
```
